32 devices in a mesh: dp: 4 (over z), adapter: 8 (over y, x, core).
Axes of the slice: x: 2, y: 2, z: 4, core: 2. Of those that a mesh axis runs over, the one named last changes fastest.
Arguments:
- states: bfloat16 [2, 1024, 8192], P(None, ('dp', 'adapter')), may hold values from -6 to 6
- request_slot_index: int32 [2, 1024, 1], P(None, ('dp', 'adapter')), may hold values from 0 to 7; in each aligned block of 32 rows (0 to 31, 32 to 63, ..., all dimensions but the last counted through in order) at most 8 rows name the same one
- down_weights: bfloat16 [32, 64, 8192], P(('dp', 'adapter')), may hold values from -0.0625 to 0.0625
- up_weights: bfloat16 [32, 64, 8192], P(('dp', 'adapter')), may hold values from -0.75 to 0.75
- active_adapter_owner: int32 [2, 8], replicated, may hold values from 0 to 3
Outputs:
- delta: bfloat16 [2, 1024, 8192], P(None, ('dp', 'adapter'))
The draws below stay inside these ranges and needn't reach their ends.
Inputs may be any that keep to these rules, and one draw needn't show every extreme that they name: `request_slot_index`: within the rows of one device at one step (aligned blocks of 32 rows), no column is named by more than 8 rows, a bound that some block reaches.
All inputs are finite; a program needn't handle non-finite values.
Results may differ from the reference program's by a relative error of at most 0.0049.
Values may be sent and summed in bfloat16 or wider, within the bound.
A program may use at most 64 MiB of HBM per device.

```python
import math
import jax
import jax.numpy as jnp
import numpy as np
from jax import lax

MODEL_DIM = 8192
ADAPTER_RANK = 64
ROWS_DEV = 32
STEPS = 2
COLS = 8
OWNERS = 4
CAP = 8
ROWS = 1024
ADAPTER_TOTAL = 32


def place_ends(values, rng, smallest, largest):
    place = [jax.random.randint(jax.random.fold_in(rng, axis), (), 0, length) for axis, length in enumerate(values.shape)]
    longest = values.shape.index(max(values.shape))
    neighbour = place[:longest] + [(place[longest] + 1) % values.shape[longest]] + place[longest + 1:]
    return values.at[tuple(place)].set(smallest).at[tuple(neighbour)].set(largest)


def level_of(rng, extent, shards, low, largest):
    loudness = 1.0
    for position, blocks in shards:
        draws = jax.random.uniform(jax.random.fold_in(jax.random.fold_in(rng, 6), position), (blocks,), jnp.float32, low / len(shards), largest / len(shards))
        loudness = loudness * jnp.repeat(jnp.exp(draws), extent[position] // blocks).reshape((-1,) + (1,) * (len(extent) - 1 - position))
    return loudness


def shared_out(rng, own, number, rows, count, top, limit, skew):
    sequence = jax.random.permutation(rng, count)
    heavy_load, common = load_shares(count, rows * top, limit, skew, True), load_shares(count, rows * top, limit, skew, False)
    places = jnp.arange(count)

    def named(sizes, rotation):
        used = int((sizes > 0).sum())
        fixed = max(1, used // 4)
        moved = fixed + (places - fixed + rotation * (used - fixed)) % max(1, count - fixed)
        return jnp.zeros((count,), jnp.int32).at[sequence[jnp.where(places < fixed, places, moved)]].set(jnp.asarray(sizes, jnp.int32))

    sizes = jnp.where(number % 4 == 0, named(heavy_load, number // 4), named(common, number - number // 4 - 1))
    mixed = jax.random.permutation(jax.random.fold_in(own, 3), count)
    donor, receiver = mixed[0:count // 2 * 2:2], mixed[1:count // 2 * 2:2]
    margin = jnp.minimum(sizes[donor] - 1, limit - sizes[receiver]) // 2
    margin = jnp.where((donor == sequence[0]) | (receiver == sequence[0]) | (sizes[receiver] == 0), 0, jnp.maximum(margin, 0))
    moved = jax.random.randint(jax.random.fold_in(own, 4), (count // 2,), 0, 1 << 20) % (margin + 1)
    sizes = sizes.at[donor].add(-moved).at[receiver].add(moved)
    members = jnp.searchsorted(jnp.cumsum(sizes), jnp.arange(rows * top), side="right").astype(jnp.int32)
    table = members.reshape(top, rows).T
    table = table[jax.random.permutation(jax.random.fold_in(own, 1), rows)]
    rotation = jax.random.randint(jax.random.fold_in(own, 2), (rows, 1), 0, top)
    return jnp.take_along_axis(table, (jnp.arange(top)[None, :] + rotation) % top, axis=1)


def load_shares(number_of, total, most, slope, full):
    loads = [(1 << 20) // math.isqrt(standing ** slope) + 1 for standing in range(1, number_of + 1)]
    largest = most if full else min(most, max(-(-total // number_of), total * loads[0] // sum(loads)))
    least = 1 if total - largest >= number_of - 1 else 0
    holding, surplus = [largest] + [least] * (number_of - 1), total - largest - least * (number_of - 1)
    while surplus > 0:
        candidates = [i for i in range(1, number_of) if holding[i] < largest] or [i for i in range(1, number_of) if holding[i] < most]
        pool, budget = sum([loads[i] for i in candidates]), surplus
        for i in candidates:
            extra = min(most - holding[i], max(1, budget * loads[i] // pool), surplus)
            holding[i] = holding[i] + extra
            surplus = surplus - extra
    return np.array(holding)


def noise(own_key, dims, width, bound, split=(), kind=jnp.bfloat16):
    values = width * jax.random.normal(own_key, dims, jnp.float32)
    if split:
        values = values * level_of(own_key, dims, split, -0.22, 0.18)
    return jnp.clip(values, -bound, bound).astype(kind)


def setup_inputs(seed: int = 0) -> dict:
    key_list = jax.random.split(jax.random.key(seed), 6)
    states = noise(key_list[0], (STEPS, ROWS, MODEL_DIM), 1.0, 6.0, ((1, 32),))
    request_slot_index_keys = jax.random.split(jax.random.fold_in(key_list[1], 1), STEPS * ROWS // ROWS_DEV)
    request_slot_index_turns = jax.random.permutation(jax.random.fold_in(key_list[1], 3), STEPS * ROWS // ROWS_DEV)
    request_slot_index = jax.vmap(lambda own, number: shared_out(jax.random.fold_in(key_list[1], 2), own, number, ROWS_DEV, COLS, 1, CAP, 2))(request_slot_index_keys, request_slot_index_turns).reshape((STEPS, ROWS, 1))
    down_weights = noise(key_list[2], (ADAPTER_TOTAL, ADAPTER_RANK, MODEL_DIM), MODEL_DIM ** -0.5, 0.0625, ((0, 32),))
    up_weights = noise(key_list[3], (ADAPTER_TOTAL, ADAPTER_RANK, MODEL_DIM), ADAPTER_RANK ** -0.5, 0.75, ((0, 32),))
    active_adapter_owner = place_ends(jax.random.randint(key_list[4], (STEPS, COLS), 0, OWNERS), jax.random.fold_in(key_list[4], 1), 0, OWNERS - 1).astype(jnp.int32)
    return dict(states=states, request_slot_index=request_slot_index, down_weights=down_weights, up_weights=up_weights, active_adapter_owner=active_adapter_owner)


def reference(states, request_slot_index, down_weights, up_weights, active_adapter_owner):
    most_rows = min(ROWS, (ROWS // ROWS_DEV) * CAP)
    per_step = []
    for step_index in range(STEPS):
        inputs = states[step_index]
        column_of_rows = request_slot_index[step_index, :, 0].astype(jnp.int32)

        def one_column(column):
            picked = jnp.argsort((column_of_rows != column).astype(jnp.int32), stable=True)[:most_rows].astype(jnp.int32)
            is_live = column_of_rows[picked] == column
            adapter_number = (active_adapter_owner[step_index, column] * COLS + column).astype(jnp.int32)
            down_weight_tile = lax.dynamic_index_in_dim(down_weights, adapter_number, 0, keepdims=False)
            up_weight_tile = lax.dynamic_index_in_dim(up_weights, adapter_number, 0, keepdims=False)
            chosen = inputs[picked]
            low_rank = lax.dot_general(chosen, down_weight_tile, (((1,), (1,)), ((), ())), preferred_element_type=jnp.float32).astype(jnp.bfloat16)
            result = jnp.dot(low_rank, up_weight_tile, preferred_element_type=jnp.float32).astype(jnp.bfloat16)
            result = jnp.where(is_live[:, None], result, jnp.zeros_like(result))
            return picked, result

        picked_all, results = lax.map(one_column, jnp.arange(COLS, dtype=jnp.int32))
        delta_rows = jnp.zeros((ROWS, MODEL_DIM), jnp.bfloat16).at[picked_all.reshape(-1)].add(results.reshape(-1, MODEL_DIM))
        per_step.append(delta_rows)
    return jnp.stack(per_step)
```

```python
import functools

import jax
import jax.numpy as jnp
from jax import lax
from jax.experimental import pallas as pl
from jax.experimental.pallas import tpu as pltpu
from jax.sharding import PartitionSpec as P

MESH = pl.DeviceIdType.MESH
F32 = jnp.float32
BF16 = jnp.bfloat16
WIDTH = 512
SKEW = 2
LAG = 2


def kernel(
    n, cols, steps, cap, block, wc,
    owner_ref, slot_ref, states_ref, down_ref, up_ref, out_ref,
    below, above, xout, arrived, dout, returned, low_acc, low, pack, unpack,
    up_send, dn_send, x_send, d_send, below_sem, above_sem, x_sem, d_sem,
):
    z = lax.axis_index("dp")
    me = lax.axis_index("adapter")
    rows = states_ref.shape[1]
    rank = down_ref.shape[1]
    nw = states_ref.shape[2] // wc
    nch = 2 * nw
    slots = cols * block
    not_first = z > 0
    not_last = z < n - 1

    def lanes(w):
        return pl.ds(pl.multiple_of(w * wc, wc), wc)

    def block_rows(j):
        return pl.ds(pl.multiple_of(j * block, block), block)

    barrier = pltpu.get_barrier_semaphore()
    for o in range(1, cols):
        pl.semaphore_signal(
            barrier, inc=1, device_id={"adapter": lax.rem(me + o, cols)}, device_id_type=MESH
        )

    @pl.when(not_first)
    def _():
        pl.semaphore_signal(barrier, inc=1, device_id={"dp": z - 1}, device_id_type=MESH)

    @pl.when(not_last)
    def _():
        pl.semaphore_signal(barrier, inc=1, device_id={"dp": z + 1}, device_id_type=MESH)

    r_sub = lax.broadcasted_iota(jnp.int32, (rows, rows), 0)
    r_lane = lax.broadcasted_iota(jnp.int32, (rows, rows), 1)
    for s in range(steps):
        crow = slot_ref[s : s + 1, :]
        crow_b = jnp.broadcast_to(crow, (rows, rows))
        ccol = jnp.sum(jnp.where(r_sub == r_lane, crow_b, 0), axis=1, keepdims=True)
        same = jnp.broadcast_to(ccol, (rows, rows)) == crow_b
        rank_row = jnp.sum(jnp.where(same & (r_sub < r_lane), 1, 0), axis=0, keepdims=True)
        rank_col = jnp.sum(jnp.where(same & (r_lane < r_sub), 1, 0), axis=1, keepdims=True)
        trow = crow * block + s * cap + rank_row
        tcol = ccol * block + s * cap + rank_col
        pack[s] = jnp.where(
            lax.broadcasted_iota(jnp.int32, (slots, rows), 0) == trow, 1.0, 0.0
        ).astype(BF16)
        unpack[s] = jnp.where(
            lax.broadcasted_iota(jnp.int32, (rows, slots), 1) == tcol, 1.0, 0.0
        ).astype(BF16)
    low_acc[...] = jnp.zeros_like(low_acc)

    owners = [owner_ref[s, me] for s in range(steps)]
    pl.semaphore_wait(
        barrier, cols - 1 + not_first.astype(jnp.int32) + not_last.astype(jnp.int32)
    )

    def put_own(buf, k, merge):
        def go(src, w):
            mine = src[0, :, lanes(w)]
            for s in range(steps):
                part = pl.ds(s * rank, rank)
                if merge:
                    buf[k, part, :] = lax.select_n(owners[s] == z, buf[k, part, :], mine)
                else:
                    buf[k, part, :] = mine

        @pl.when(k < nw)
        def _():
            go(down_ref, k)

        @pl.when(k >= nw)
        def _():
            go(up_ref, k - nw)

    def hop(buf, k, has_in, has_out, target, recv_sem, send_sem):
        copy = pltpu.make_async_remote_copy(
            src_ref=buf.at[k],
            dst_ref=buf.at[k],
            send_sem=send_sem,
            recv_sem=recv_sem.at[k],
            device_id={"dp": target},
            device_id_type=MESH,
        )

        @pl.when(has_in)
        def _():
            copy.wait_recv()
            put_own(buf, k, True)

        @pl.when(jnp.logical_not(has_in))
        def _():
            put_own(buf, k, False)

        @pl.when(has_out)
        def _():
            copy.start()

    def exchange(src, dst, w, send_sem, recv_sem):
        dst[w, block_rows(me), :] = src[w, block_rows(me), :]
        for o in range(1, cols):
            peer = lax.rem(me + o, cols)
            pltpu.make_async_remote_copy(
                src_ref=src.at[w, block_rows(peer)],
                dst_ref=dst.at[w, block_rows(me)],
                send_sem=send_sem,
                recv_sem=recv_sem.at[w],
                device_id={"adapter": peer},
                device_id_type=MESH,
            ).start()

    def wait_exchange(dst, w, recv_sem):
        part = dst.at[w, pl.ds(0, slots - block)]
        pltpu.make_async_copy(part, part, recv_sem.at[w]).wait()

    def chosen(k):
        parts = []
        for s in range(steps):
            part = pl.ds(s * rank, rank)
            parts.append(lax.select_n(owners[s] <= z, above[k, part, :], below[k, part, :]))
        return jnp.concatenate(parts, axis=0)

    def iteration(i, carry):
        k_up = i - SKEW * z
        k_dn = i - SKEW * (n - 1 - z)

        @pl.when((k_up >= 0) & (k_up < nch))
        def _():
            hop(below, k_up, not_first, not_last, lax.rem(z + 1, n), below_sem, up_send)

        @pl.when((k_dn >= 0) & (k_dn < nch))
        def _():
            hop(above, k_dn, not_last, not_first, lax.rem(z + n - 1, n), above_sem, dn_send)

        @pl.when(i < nw)
        def _():
            total = jnp.zeros((slots, wc), F32)
            for s in range(steps):
                total = total + jnp.dot(
                    pack[s], states_ref[s, :, lanes(i)], preferred_element_type=F32
                )
            xout[i] = total.astype(BF16)
            exchange(xout, arrived, i, x_send, x_sem)

        k = i - SKEW * (n - 1)

        @pl.when((k >= 0) & (k < nw))
        def _():
            wait_exchange(arrived, k, x_sem)
            low_acc[...] += lax.dot_general(
                arrived[k], chosen(k), (((1,), (1,)), ((), ())), preferred_element_type=F32
            )

        @pl.when(k == nw - 1)
        def _():
            of_row = lax.rem(lax.broadcasted_iota(jnp.int32, low.shape, 0), block) // cap
            of_col = lax.broadcasted_iota(jnp.int32, low.shape, 1) // rank
            low[...] = jnp.where(of_row == of_col, low_acc[...], 0.0).astype(BF16)

        @pl.when((k >= nw) & (k < nch))
        def _():
            w = k - nw
            dout[w] = jnp.dot(low[...], chosen(k), preferred_element_type=F32).astype(BF16)
            exchange(dout, returned, w, d_send, d_sem)

        w_out = k - nw - LAG

        @pl.when((w_out >= 0) & (w_out < nw))
        def _():
            wait_exchange(returned, w_out, d_sem)
            for s in range(steps):
                out_ref[s, :, lanes(w_out)] = jnp.dot(
                    unpack[s], returned[w_out], preferred_element_type=F32
                ).astype(BF16)

        return carry

    lax.fori_loop(0, nch + SKEW * (n - 1) + LAG, iteration, 0)

    @pl.when(not_last)
    def _():
        pltpu.make_async_copy(below, below, up_send).wait()

    @pl.when(not_first)
    def _():
        pltpu.make_async_copy(above, above, dn_send).wait()

    for buf, sem in ((xout, x_send), (dout, d_send)):
        part = buf.at[:, pl.ds(0, slots - block)]
        pltpu.make_async_copy(part, part, sem).wait()


def body(n, cols, states, request_slot_index, down_weights, up_weights, active_adapter_owner):
    steps, rows, width = states.shape
    rank = down_weights.shape[1]
    cap = max(2, 2 * rows // cols)
    block = -(-steps * cap // 16) * 16
    slots = cols * block
    wc = min(WIDTH, width)
    nw = width // wc
    vmem = pl.BlockSpec(memory_space=pltpu.VMEM)
    dma = pltpu.SemaphoreType.DMA
    return pl.pallas_call(
        functools.partial(kernel, n, cols, steps, cap, block, wc),
        out_shape=jax.ShapeDtypeStruct(states.shape, states.dtype),
        in_specs=[pl.BlockSpec(memory_space=pltpu.SMEM)] + [vmem] * 4,
        out_specs=vmem,
        scratch_shapes=[
            pltpu.VMEM((2 * nw, steps * rank, wc), BF16),
            pltpu.VMEM((2 * nw, steps * rank, wc), BF16),
            pltpu.VMEM((nw, slots, wc), BF16),
            pltpu.VMEM((nw, slots, wc), BF16),
            pltpu.VMEM((nw, slots, wc), BF16),
            pltpu.VMEM((nw, slots, wc), BF16),
            pltpu.VMEM((slots, steps * rank), F32),
            pltpu.VMEM((slots, steps * rank), BF16),
            pltpu.VMEM((steps, slots, rows), BF16),
            pltpu.VMEM((steps, rows, slots), BF16),
            dma, dma, dma, dma,
            dma((2 * nw,)), dma((2 * nw,)), dma((nw,)), dma((nw,)),
        ],
        compiler_params=pltpu.CompilerParams(
            collective_id=0, has_side_effects=True, vmem_limit_bytes=56 * 1024 * 1024
        ),
    )(active_adapter_owner, request_slot_index[:, :, 0], states, down_weights, up_weights)


def solution(mesh):
    return jax.shard_map(
        functools.partial(body, mesh.shape["dp"], mesh.shape["adapter"]),
        mesh=mesh,
        in_specs=(
            P(None, ("dp", "adapter"), None),
            P(None, ("dp", "adapter"), None),
            P(("dp", "adapter"), None, None),
            P(("dp", "adapter"), None, None),
            P(),
        ),
        out_specs=P(None, ("dp", "adapter"), None),
        check_vma=False,
    )
```

```python
import functools

import jax
import jax.numpy as jnp
from jax import lax
from jax.experimental import pallas as pl
from jax.experimental.pallas import tpu as pltpu
from jax.sharding import PartitionSpec as P

MESH = pl.DeviceIdType.MESH
F32 = jnp.float32
BF16 = jnp.bfloat16
WIDTH = 256
SKEW = 3
LAG = 2
GROUP = 2


def kernel(
    n, cols, steps, cap, block, wc, group,
    owner_ref, slot_ref, states_any, down_any, up_any, out_ref,
    states_ref, down_ref, up_ref, below, above, xout, arrived, dout, returned, low_acc, low, pack, unpack,
    in_sem, up_send, dn_send, x_send, d_send, below_sem, above_sem, x_sem, d_sem,
):
    z = lax.axis_index("dp")
    me = lax.axis_index("adapter")
    rows = states_any.shape[1]
    rank = down_any.shape[1]
    nw = states_any.shape[2] // wc
    nch = 2 * nw
    slots = cols * block
    not_first = z > 0
    not_last = z < n - 1

    pieces = nw // group
    pw = wc * group
    loads = [
        pltpu.make_async_copy(src, dst, in_sem.at[i])
        for i, (src, dst) in enumerate(
            ((down_any, down_ref), (up_any, up_ref), (states_any, states_ref))
        )
    ]
    for load in loads:
        load.start()

    def lanes(w):
        return pl.ds(pl.multiple_of(w * wc, wc), wc)

    def piece_lanes(p):
        return pl.ds(pl.multiple_of(p * pw, pw), pw)

    def block_rows(j):
        return pl.ds(pl.multiple_of(j * block, block), block)

    barrier = pltpu.get_barrier_semaphore()
    for o in range(1, cols):
        pl.semaphore_signal(
            barrier, inc=1, device_id={"adapter": lax.rem(me + o, cols)}, device_id_type=MESH
        )

    @pl.when(not_first)
    def _():
        pl.semaphore_signal(barrier, inc=1, device_id={"dp": z - 1}, device_id_type=MESH)

    @pl.when(not_last)
    def _():
        pl.semaphore_signal(barrier, inc=1, device_id={"dp": z + 1}, device_id_type=MESH)

    r_sub = lax.broadcasted_iota(jnp.int32, (rows, rows), 0)
    r_lane = lax.broadcasted_iota(jnp.int32, (rows, rows), 1)
    for s in range(steps):
        crow = slot_ref[s : s + 1, :]
        crow_b = jnp.broadcast_to(crow, (rows, rows))
        ccol = jnp.sum(jnp.where(r_sub == r_lane, crow_b, 0), axis=1, keepdims=True)
        same = jnp.broadcast_to(ccol, (rows, rows)) == crow_b
        rank_row = jnp.sum(jnp.where(same & (r_sub < r_lane), 1, 0), axis=0, keepdims=True)
        rank_col = jnp.sum(jnp.where(same & (r_lane < r_sub), 1, 0), axis=1, keepdims=True)
        trow = crow * block + s * cap + rank_row
        tcol = ccol * block + s * cap + rank_col
        pack[s] = jnp.where(
            lax.broadcasted_iota(jnp.int32, (slots, rows), 0) == trow, 1.0, 0.0
        ).astype(BF16)
        unpack[s] = jnp.where(
            lax.broadcasted_iota(jnp.int32, (rows, slots), 1) == tcol, 1.0, 0.0
        ).astype(BF16)
    low_acc[...] = jnp.zeros_like(low_acc)

    owners = [owner_ref[s, me] for s in range(steps)]
    for load in loads:
        load.wait()
    pl.semaphore_wait(
        barrier, cols - 1 + not_first.astype(jnp.int32) + not_last.astype(jnp.int32)
    )

    def own(k, use):
        @pl.when(k < nw)
        def _():
            use(down_ref[0, :, lanes(k)])

        @pl.when(k >= nw)
        def _():
            use(up_ref[0, :, lanes(k - nw)])

    def part(s):
        return pl.ds(s * rank, rank)

    def hop(buf, i, place, owner_places, target, recv_sem, send_sem):
        def copy(k, src, dst):
            return pltpu.make_async_remote_copy(
                src_ref=buf.at[k, src],
                dst_ref=buf.at[k, dst],
                send_sem=send_sem,
                recv_sem=recv_sem.at[k],
                device_id={"dp": target},
                device_id_type=MESH,
            )

        whole = pl.ds(0, steps * rank)
        second = i - SKEW
        later = i - SKEW * place

        @pl.when((place == 0) & (i < nch))
        def _():
            def use(mine):
                for s in range(steps):
                    buf[i, part(s), :] = mine

            own(i, use)
            copy(i, part(0), part(1)).start()

        @pl.when((place == 1) & (i < nch))
        def _():
            def use(mine):
                buf[i, part(0), :] = mine

            own(i, use)

            @pl.when(place < n - 1)
            def _():
                copy(i, part(0), part(0)).start()

        @pl.when((place == 1) & (second >= 0) & (second < nch))
        def _():
            copy(second, part(1), part(1)).wait_recv()

            @pl.when(place < n - 1)
            def _():
                copy(second, part(1), part(1)).start()

        @pl.when((place > 1) & (later >= 0) & (later < nch))
        def _():
            copy(later, whole, whole).wait_recv()

            def use(mine):
                theirs = [buf[later, part(s), :] for s in range(steps)]
                for s in range(steps):
                    value = theirs[s]
                    raw = place == 2
                    if s == 0:
                        value = lax.select_n(raw & (owner_places[s] == 0), value, theirs[1])
                    else:
                        value = lax.select_n(raw & (owner_places[s] == 0), value, theirs[1])
                        value = lax.select_n(raw & (owner_places[s] == 1), value, theirs[0])
                    buf[later, part(s), :] = lax.select_n(owner_places[s] == place, value, mine)

            own(later, use)

            @pl.when(place < n - 1)
            def _():
                copy(later, whole, whole).start()

    def wait_sent(buf, place, send_sem):
        @pl.when(place == 0)
        def _():
            sent = buf.at[:, part(0)]
            pltpu.make_async_copy(sent, sent, send_sem).wait()

        @pl.when((place > 0) & (place < n - 1))
        def _():
            pltpu.make_async_copy(buf, buf, send_sem).wait()

    def exchange(src, dst, w, send_sem, recv_sem):
        dst[w, block_rows(me), :] = src[w, block_rows(me), :]
        for o in range(1, cols):
            peer = lax.rem(me + o, cols)
            pltpu.make_async_remote_copy(
                src_ref=src.at[w, block_rows(peer)],
                dst_ref=dst.at[w, block_rows(me)],
                send_sem=send_sem,
                recv_sem=recv_sem.at[w],
                device_id={"adapter": peer},
                device_id_type=MESH,
            ).start()

    def wait_exchange(dst, w, recv_sem):
        remote = dst.at[w, pl.ds(0, slots - block)]
        pltpu.make_async_copy(remote, remote, recv_sem.at[w]).wait()

    ups = owners
    dns = [n - 1 - owner for owner in owners]

    def pick(buf, k, place, owner_places, s):
        other = (place == 1) & (owner_places[s] == (0 if s == 0 else 1))
        return lax.select_n(other, buf[k, part(s), :], buf[k, part(1 if s == 0 else 0), :])

    def chosen(k):
        parts = []
        for s in range(steps):
            parts.append(
                lax.select_n(
                    owners[s] <= z,
                    pick(above, k, n - 1 - z, dns, s),
                    pick(below, k, z, ups, s),
                )
            )
        return jnp.concatenate(parts, axis=0)

    def iteration(i, carry):
        hop(below, i, z, ups, lax.rem(z + 1, n), below_sem, up_send)
        hop(above, i, n - 1 - z, dns, lax.rem(z + n - 1, n), above_sem, dn_send)

        @pl.when((lax.rem(i, group) == 0) & (i < nw))
        def _():
            p = i // group
            total = jnp.zeros((slots, pw), F32)
            for s in range(steps):
                total = total + jnp.dot(
                    pack[s], states_ref[s, :, piece_lanes(p)], preferred_element_type=F32
                )
            xout[p] = total.astype(BF16)
            exchange(xout, arrived, p, x_send, x_sem)

        k = i - SKEW * (n - 1)

        @pl.when((k >= 0) & (k < nw) & (lax.rem(k, group) == 0))
        def _():
            wait_exchange(arrived, k // group, x_sem)

        @pl.when((k >= 0) & (k < nw))
        def _():
            low_acc[...] += lax.dot_general(
                arrived[k // group, :, lanes(lax.rem(k, group))],
                chosen(k),
                (((1,), (1,)), ((), ())),
                preferred_element_type=F32,
            )

        @pl.when(k == nw - 1)
        def _():
            of_row = lax.rem(lax.broadcasted_iota(jnp.int32, low.shape, 0), block) // cap
            of_col = lax.broadcasted_iota(jnp.int32, low.shape, 1) // rank
            low[...] = jnp.where(of_row == of_col, low_acc[...], 0.0).astype(BF16)

        @pl.when((k >= nw) & (k < nch))
        def _():
            w = k - nw
            dout[w // group, :, lanes(lax.rem(w, group))] = jnp.dot(
                low[...], chosen(k), preferred_element_type=F32
            ).astype(BF16)

        @pl.when((k >= nw) & (k < nch) & (lax.rem(k - nw, group) == group - 1))
        def _():
            exchange(dout, returned, (k - nw) // group, d_send, d_sem)

        w_out = k - nw - LAG

        @pl.when((w_out >= 0) & (w_out < nw) & (lax.rem(w_out, group) == group - 1))
        def _():
            p = w_out // group
            wait_exchange(returned, p, d_sem)
            for s in range(steps):
                out_ref[s, :, piece_lanes(p)] = jnp.dot(
                    unpack[s], returned[p], preferred_element_type=F32
                ).astype(BF16)

        return carry

    lax.fori_loop(0, nch + SKEW * (n - 1) + LAG, iteration, 0)

    wait_sent(below, z, up_send)
    wait_sent(above, n - 1 - z, dn_send)
    for buf, sem in ((xout, x_send), (dout, d_send)):
        sent = buf.at[:, pl.ds(0, slots - block)]
        pltpu.make_async_copy(sent, sent, sem).wait()


def body(n, cols, states, request_slot_index, down_weights, up_weights, active_adapter_owner):
    steps, rows, width = states.shape
    rank = down_weights.shape[1]
    cap = max(2, 2 * rows // cols)
    block = -(-steps * cap // 16) * 16
    slots = cols * block
    wc = min(WIDTH, width)
    nw = width // wc
    group = GROUP if nw % GROUP == 0 else 1
    vmem = pl.BlockSpec(memory_space=pltpu.VMEM)
    hbm = pl.BlockSpec(memory_space=pl.ANY)
    dma = pltpu.SemaphoreType.DMA
    stream = pltpu.VMEM((2 * nw, steps * rank, wc), BF16)
    piece = pltpu.VMEM((nw // group, slots, wc * group), BF16)
    return pl.pallas_call(
        functools.partial(kernel, n, cols, steps, cap, block, wc, group),
        out_shape=pltpu.VMEM(states.shape, states.dtype),
        in_specs=[pl.BlockSpec(memory_space=pltpu.SMEM), vmem, hbm, hbm, hbm],
        out_specs=vmem,
        scratch_shapes=[
            pltpu.VMEM(states.shape, BF16),
            pltpu.VMEM(down_weights.shape, BF16),
            pltpu.VMEM(up_weights.shape, BF16),
            stream, stream, piece, piece, piece, piece,
            pltpu.VMEM((slots, steps * rank), F32),
            pltpu.VMEM((slots, steps * rank), BF16),
            pltpu.VMEM((steps, slots, rows), BF16),
            pltpu.VMEM((steps, rows, slots), BF16),
            dma((3,)), dma, dma, dma, dma,
            dma((2 * nw,)), dma((2 * nw,)), dma((nw // group,)), dma((nw // group,)),
        ],
        compiler_params=pltpu.CompilerParams(
            collective_id=0, has_side_effects=True, vmem_limit_bytes=56 * 1024 * 1024
        ),
    )(active_adapter_owner, request_slot_index[:, :, 0], states, down_weights, up_weights)


def solution(mesh):
    return jax.shard_map(
        functools.partial(body, mesh.shape["dp"], mesh.shape["adapter"]),
        mesh=mesh,
        in_specs=(
            P(None, ("dp", "adapter"), None),
            P(None, ("dp", "adapter"), None),
            P(("dp", "adapter"), None, None),
            P(("dp", "adapter"), None, None),
            P(),
        ),
        out_specs=P(None, ("dp", "adapter"), None),
        check_vma=False,
    )
```

```python
import functools

import jax
import jax.numpy as jnp
from jax import lax
from jax.experimental import pallas as pl
from jax.experimental.pallas import tpu as pltpu
from jax.sharding import PartitionSpec as P

MESH = pl.DeviceIdType.MESH
F32 = jnp.float32
BF16 = jnp.bfloat16
WIDTH = 256
SKEW = 3
LAG = 3
GROUP = 2


def kernel(
    n, cols, steps, cap, block, wc, group,
    owner_ref, slot_ref, states_any, down_any, up_any, out_ref,
    states_ref, down_ref, up_ref, below, above, xout, arrived, dout, returned, low_acc, low, pack, unpack,
    in_sem, up_send, dn_send, x_send, d_send, below_sem, above_sem, x_sem, d_sem,
):
    z = lax.axis_index("dp")
    me = lax.axis_index("adapter")
    rows = states_any.shape[1]
    rank = down_any.shape[1]
    nw = states_any.shape[2] // wc
    nch = 2 * nw
    slots = cols * block
    not_first = z > 0
    not_last = z < n - 1

    pieces = nw // group
    pw = wc * group
    loads = [
        pltpu.make_async_copy(src, dst, in_sem.at[i])
        for i, (src, dst) in enumerate(
            ((down_any, down_ref), (up_any, up_ref), (states_any, states_ref))
        )
    ]
    for load in loads:
        load.start()

    def lanes(w):
        return pl.ds(pl.multiple_of(w * wc, wc), wc)

    def piece_lanes(p):
        return pl.ds(pl.multiple_of(p * pw, pw), pw)

    def block_rows(j):
        return pl.ds(pl.multiple_of(j * block, block), block)

    barrier = pltpu.get_barrier_semaphore()
    for o in range(1, cols):
        pl.semaphore_signal(
            barrier, inc=1, device_id={"adapter": lax.rem(me + o, cols)}, device_id_type=MESH
        )

    @pl.when(not_first)
    def _():
        pl.semaphore_signal(barrier, inc=1, device_id={"dp": z - 1}, device_id_type=MESH)

    @pl.when(not_last)
    def _():
        pl.semaphore_signal(barrier, inc=1, device_id={"dp": z + 1}, device_id_type=MESH)

    r_sub = lax.broadcasted_iota(jnp.int32, (rows, rows), 0)
    r_lane = lax.broadcasted_iota(jnp.int32, (rows, rows), 1)
    for s in range(steps):
        crow = slot_ref[s : s + 1, :]
        crow_b = jnp.broadcast_to(crow, (rows, rows))
        ccol = jnp.sum(jnp.where(r_sub == r_lane, crow_b, 0), axis=1, keepdims=True)
        same = jnp.broadcast_to(ccol, (rows, rows)) == crow_b
        rank_row = jnp.sum(jnp.where(same & (r_sub < r_lane), 1, 0), axis=0, keepdims=True)
        rank_col = jnp.sum(jnp.where(same & (r_lane < r_sub), 1, 0), axis=1, keepdims=True)
        trow = crow * block + s * cap + rank_row
        tcol = ccol * block + s * cap + rank_col
        pack[s] = jnp.where(
            lax.broadcasted_iota(jnp.int32, (slots, rows), 0) == trow, 1.0, 0.0
        ).astype(BF16)
        unpack[s] = jnp.where(
            lax.broadcasted_iota(jnp.int32, (rows, slots), 1) == tcol, 1.0, 0.0
        ).astype(BF16)
    low_acc[...] = jnp.zeros_like(low_acc)

    owners = [owner_ref[s, me] for s in range(steps)]
    for load in loads:
        load.wait()
    pl.semaphore_wait(
        barrier, cols - 1 + not_first.astype(jnp.int32) + not_last.astype(jnp.int32)
    )

    def own(k, use):
        @pl.when(k < nw)
        def _():
            use(down_ref[0, :, lanes(k)])

        @pl.when(k >= nw)
        def _():
            use(up_ref[0, :, lanes(k - nw)])

    def part(s):
        return pl.ds(s * rank, rank)

    def hop(buf, i, place, owner_places, target, recv_sem, send_sem):
        def copy(k, src, dst):
            return pltpu.make_async_remote_copy(
                src_ref=buf.at[k, src],
                dst_ref=buf.at[k, dst],
                send_sem=send_sem,
                recv_sem=recv_sem.at[k],
                device_id={"dp": target},
                device_id_type=MESH,
            )

        whole = pl.ds(0, steps * rank)
        second = i - SKEW
        later = i - SKEW * place

        @pl.when((place == 0) & (i < nch))
        def _():
            def use(mine):
                for s in range(steps):
                    buf[i, part(s), :] = mine

            own(i, use)
            copy(i, part(0), part(1)).start()

        @pl.when((place == 1) & (i < nch))
        def _():
            def use(mine):
                buf[i, part(0), :] = mine

            own(i, use)

            @pl.when(place < n - 1)
            def _():
                copy(i, part(0), part(0)).start()

        @pl.when((place == 1) & (second >= 0) & (second < nch))
        def _():
            copy(second, part(1), part(1)).wait_recv()

            @pl.when(place < n - 1)
            def _():
                copy(second, part(1), part(1)).start()

        @pl.when((place > 1) & (later >= 0) & (later < nch))
        def _():
            copy(later, whole, whole).wait_recv()

            def use(mine):
                theirs = [buf[later, part(s), :] for s in range(steps)]
                for s in range(steps):
                    value = theirs[s]
                    raw = place == 2
                    if s == 0:
                        value = lax.select_n(raw & (owner_places[s] == 0), value, theirs[1])
                    else:
                        value = lax.select_n(raw & (owner_places[s] == 0), value, theirs[1])
                        value = lax.select_n(raw & (owner_places[s] == 1), value, theirs[0])
                    buf[later, part(s), :] = lax.select_n(owner_places[s] == place, value, mine)

            own(later, use)

            @pl.when(place < n - 1)
            def _():
                copy(later, whole, whole).start()

    def wait_sent(buf, place, send_sem):
        @pl.when(place == 0)
        def _():
            sent = buf.at[:, part(0)]
            pltpu.make_async_copy(sent, sent, send_sem).wait()

        @pl.when((place > 0) & (place < n - 1))
        def _():
            pltpu.make_async_copy(buf, buf, send_sem).wait()

    partners = []
    for o in range(cols - 1, 0, -1):
        peer, bit = 0, 1
        while bit < cols:
            peer = peer + bit * lax.rem(lax.rem(me // bit, 2) + o // bit % 2, 2)
            bit = 2 * bit
        partners.append(peer if bit == cols else lax.rem(me + o, cols))

    def exchange(src, dst, w, send_sem, recv_sem):
        for peer in partners:
            pltpu.make_async_remote_copy(
                src_ref=src.at[w, block_rows(peer)],
                dst_ref=dst.at[w, block_rows(me)],
                send_sem=send_sem,
                recv_sem=recv_sem.at[w],
                device_id={"adapter": peer},
                device_id_type=MESH,
            ).start()
        dst[w, block_rows(me), :] = src[w, block_rows(me), :]

    def wait_exchange(dst, w, recv_sem):
        remote = dst.at[w, pl.ds(0, slots - block)]
        pltpu.make_async_copy(remote, remote, recv_sem.at[w]).wait()

    ups = owners
    dns = [n - 1 - owner for owner in owners]

    def pick(buf, k, place, owner_places, s):
        other = (place == 1) & (owner_places[s] == (0 if s == 0 else 1))
        return lax.select_n(other, buf[k, part(s), :], buf[k, part(1 if s == 0 else 0), :])

    def chosen(k):
        parts = []
        for s in range(steps):
            parts.append(
                lax.select_n(
                    owners[s] <= z,
                    pick(above, k, n - 1 - z, dns, s),
                    pick(below, k, z, ups, s),
                )
            )
        return jnp.concatenate(parts, axis=0)

    def iteration(i, carry):
        hop(below, i, z, ups, lax.rem(z + 1, n), below_sem, up_send)
        hop(above, i, n - 1 - z, dns, lax.rem(z + n - 1, n), above_sem, dn_send)

        @pl.when((lax.rem(i, group) == 0) & (i < nw))
        def _():
            p = i // group
            total = jnp.zeros((slots, pw), F32)
            for s in range(steps):
                total = total + jnp.dot(
                    pack[s], states_ref[s, :, piece_lanes(p)], preferred_element_type=F32
                )
            xout[p] = total.astype(BF16)
            exchange(xout, arrived, p, x_send, x_sem)

        k = i - SKEW * (n - 1)

        @pl.when((k >= 0) & (k < nw) & (lax.rem(k, group) == 0))
        def _():
            wait_exchange(arrived, k // group, x_sem)

        @pl.when((k >= 0) & (k < nw))
        def _():
            low_acc[...] += lax.dot_general(
                arrived[k // group, :, lanes(lax.rem(k, group))],
                chosen(k),
                (((1,), (1,)), ((), ())),
                preferred_element_type=F32,
            )

        @pl.when(k == nw - 1)
        def _():
            of_row = lax.rem(lax.broadcasted_iota(jnp.int32, low.shape, 0), block) // cap
            of_col = lax.broadcasted_iota(jnp.int32, low.shape, 1) // rank
            low[...] = jnp.where(of_row == of_col, low_acc[...], 0.0).astype(BF16)

        @pl.when((k >= nw) & (k < nch))
        def _():
            w = k - nw
            dout[w // group, :, lanes(lax.rem(w, group))] = jnp.dot(
                low[...], chosen(k), preferred_element_type=F32
            ).astype(BF16)

        @pl.when((k >= nw) & (k < nch) & (lax.rem(k - nw, group) == group - 1))
        def _():
            exchange(dout, returned, (k - nw) // group, d_send, d_sem)

        w_out = k - nw - LAG

        @pl.when((w_out >= 0) & (w_out < nw) & (lax.rem(w_out, group) == group - 1))
        def _():
            p = w_out // group
            wait_exchange(returned, p, d_sem)
            for s in range(steps):
                out_ref[s, :, piece_lanes(p)] = jnp.dot(
                    unpack[s], returned[p], preferred_element_type=F32
                ).astype(BF16)

        return carry

    lax.fori_loop(0, nch + SKEW * (n - 1) + LAG, iteration, 0)

    wait_sent(below, z, up_send)
    wait_sent(above, n - 1 - z, dn_send)
    for buf, sem in ((xout, x_send), (dout, d_send)):
        sent = buf.at[:, pl.ds(0, slots - block)]
        pltpu.make_async_copy(sent, sent, sem).wait()


def body(n, cols, states, request_slot_index, down_weights, up_weights, active_adapter_owner):
    steps, rows, width = states.shape
    rank = down_weights.shape[1]
    cap = max(2, 2 * rows // cols)
    block = -(-steps * cap // 16) * 16
    slots = cols * block
    wc = min(WIDTH, width)
    nw = width // wc
    group = GROUP if nw % GROUP == 0 else 1
    vmem = pl.BlockSpec(memory_space=pltpu.VMEM)
    hbm = pl.BlockSpec(memory_space=pl.ANY)
    dma = pltpu.SemaphoreType.DMA
    stream = pltpu.VMEM((2 * nw, steps * rank, wc), BF16)
    piece = pltpu.VMEM((nw // group, slots, wc * group), BF16)
    return pl.pallas_call(
        functools.partial(kernel, n, cols, steps, cap, block, wc, group),
        out_shape=pltpu.VMEM(states.shape, states.dtype),
        in_specs=[pl.BlockSpec(memory_space=pltpu.SMEM), vmem, hbm, hbm, hbm],
        out_specs=vmem,
        scratch_shapes=[
            pltpu.VMEM(states.shape, BF16),
            pltpu.VMEM(down_weights.shape, BF16),
            pltpu.VMEM(up_weights.shape, BF16),
            stream, stream, piece, piece, piece, piece,
            pltpu.VMEM((slots, steps * rank), F32),
            pltpu.VMEM((slots, steps * rank), BF16),
            pltpu.VMEM((steps, slots, rows), BF16),
            pltpu.VMEM((steps, rows, slots), BF16),
            dma((3,)), dma, dma, dma, dma,
            dma((2 * nw,)), dma((2 * nw,)), dma((nw // group,)), dma((nw // group,)),
        ],
        compiler_params=pltpu.CompilerParams(
            collective_id=0, has_side_effects=True, vmem_limit_bytes=56 * 1024 * 1024
        ),
    )(active_adapter_owner, request_slot_index[:, :, 0], states, down_weights, up_weights)


def solution(mesh):
    return jax.shard_map(
        functools.partial(body, mesh.shape["dp"], mesh.shape["adapter"]),
        mesh=mesh,
        in_specs=(
            P(None, ("dp", "adapter"), None),
            P(None, ("dp", "adapter"), None),
            P(("dp", "adapter"), None, None),
            P(("dp", "adapter"), None, None),
            P(),
        ),
        out_specs=P(None, ("dp", "adapter"), None),
        check_vma=False,
    )
```

```python
import functools

import jax
import jax.numpy as jnp
from jax import lax
from jax.experimental import pallas as pl
from jax.experimental.pallas import tpu as pltpu
from jax.sharding import PartitionSpec as P

MESH = pl.DeviceIdType.MESH
F32 = jnp.float32
BF16 = jnp.bfloat16
WIDTH = 256
SKEW = 3
LAG = 3
GROUP = 2


def kernel(
    n, cols, steps, cap, block, wc, group,
    owner_ref, slot_ref, states_any, down_any, up_any, out_ref,
    states_ref, down_ref, up_ref, below, above, xout, arrived, dout, returned, low_acc, low, pack, unpack,
    in_sem, up_send, dn_send, x_send, d_send, below_sem, above_sem, x_sem, d_sem,
):
    z = lax.axis_index("dp")
    me = lax.axis_index("adapter")
    rows = states_any.shape[1]
    rank = down_any.shape[1]
    nw = states_any.shape[2] // wc
    nch = 2 * nw
    slots = cols * block
    not_first = z > 0
    not_last = z < n - 1

    pieces = nw // group
    pw = wc * group
    loads = [
        pltpu.make_async_copy(src, dst, in_sem.at[i])
        for i, (src, dst) in enumerate(
            ((down_any, down_ref), (up_any, up_ref), (states_any, states_ref))
        )
    ]
    for load in loads:
        load.start()

    def lanes(w):
        return pl.ds(pl.multiple_of(w * wc, wc), wc)

    def piece_lanes(p):
        return pl.ds(pl.multiple_of(p * pw, pw), pw)

    def block_rows(j):
        return pl.ds(pl.multiple_of(j * block, block), block)

    barrier = pltpu.get_barrier_semaphore()
    for o in range(1, cols):
        pl.semaphore_signal(
            barrier, inc=1, device_id={"adapter": lax.rem(me + o, cols)}, device_id_type=MESH
        )

    @pl.when(not_first)
    def _():
        pl.semaphore_signal(barrier, inc=1, device_id={"dp": z - 1}, device_id_type=MESH)

    @pl.when(not_last)
    def _():
        pl.semaphore_signal(barrier, inc=1, device_id={"dp": z + 1}, device_id_type=MESH)

    r_sub = lax.broadcasted_iota(jnp.int32, (rows, rows), 0)
    r_lane = lax.broadcasted_iota(jnp.int32, (rows, rows), 1)
    for s in range(steps):
        crow = slot_ref[s : s + 1, :]
        crow_b = jnp.broadcast_to(crow, (rows, rows))
        ccol = jnp.sum(jnp.where(r_sub == r_lane, crow_b, 0), axis=1, keepdims=True)
        same = jnp.broadcast_to(ccol, (rows, rows)) == crow_b
        rank_row = jnp.sum(jnp.where(same & (r_sub < r_lane), 1, 0), axis=0, keepdims=True)
        rank_col = jnp.sum(jnp.where(same & (r_lane < r_sub), 1, 0), axis=1, keepdims=True)
        trow = crow * block + s * cap + rank_row
        tcol = ccol * block + s * cap + rank_col
        pack[s] = jnp.where(
            lax.broadcasted_iota(jnp.int32, (slots, rows), 0) == trow, 1.0, 0.0
        ).astype(BF16)
        unpack[s] = jnp.where(
            lax.broadcasted_iota(jnp.int32, (rows, slots), 1) == tcol, 1.0, 0.0
        ).astype(BF16)
    low_acc[...] = jnp.zeros_like(low_acc)

    owners = [owner_ref[s, me] for s in range(steps)]
    for load in loads:
        load.wait()
    pl.semaphore_wait(
        barrier, cols - 1 + not_first.astype(jnp.int32) + not_last.astype(jnp.int32)
    )

    def own(k, use):
        @pl.when(k < nw)
        def _():
            use(down_ref[0, :, lanes(k)])

        @pl.when(k >= nw)
        def _():
            use(up_ref[0, :, lanes(k - nw)])

    def part(s):
        return pl.ds(s * rank, rank)

    def hop(buf, i, place, owner_places, target, recv_sem, send_sem):
        def copy(k, src, dst):
            return pltpu.make_async_remote_copy(
                src_ref=buf.at[k, src],
                dst_ref=buf.at[k, dst],
                send_sem=send_sem,
                recv_sem=recv_sem.at[k],
                device_id={"dp": target},
                device_id_type=MESH,
            )

        whole = pl.ds(0, steps * rank)
        second = i - SKEW
        later = i - SKEW * place

        @pl.when((place == 0) & (i < nch))
        def _():
            def use(mine):
                for s in range(steps):
                    buf[i, part(s), :] = mine

            own(i, use)
            copy(i, part(0), part(1)).start()

        @pl.when((place == 1) & (i < nch))
        def _():
            def use(mine):
                buf[i, part(0), :] = mine

            own(i, use)

            @pl.when(place < n - 1)
            def _():
                copy(i, part(0), part(0)).start()

        @pl.when((place == 1) & (second >= 0) & (second < nch))
        def _():
            copy(second, part(1), part(1)).wait_recv()

            @pl.when(place < n - 1)
            def _():
                copy(second, part(1), part(1)).start()

        @pl.when((place > 1) & (later >= 0) & (later < nch))
        def _():
            copy(later, whole, whole).wait_recv()

            def use(mine):
                theirs = [buf[later, part(s), :] for s in range(steps)]
                for s in range(steps):
                    value = theirs[s]
                    raw = place == 2
                    if s == 0:
                        value = lax.select_n(raw & (owner_places[s] == 0), value, theirs[1])
                    else:
                        value = lax.select_n(raw & (owner_places[s] == 0), value, theirs[1])
                        value = lax.select_n(raw & (owner_places[s] == 1), value, theirs[0])
                    buf[later, part(s), :] = lax.select_n(owner_places[s] == place, value, mine)

            own(later, use)

            @pl.when(place < n - 1)
            def _():
                copy(later, whole, whole).start()

    def wait_sent(buf, place, send_sem):
        @pl.when(place == 0)
        def _():
            sent = buf.at[:, part(0)]
            pltpu.make_async_copy(sent, sent, send_sem).wait()

        @pl.when((place > 0) & (place < n - 1))
        def _():
            pltpu.make_async_copy(buf, buf, send_sem).wait()

    partners = []
    for o in range(cols - 1, 0, -1):
        peer, bit = 0, 1
        while bit < cols:
            peer = peer + bit * lax.rem(lax.rem(me // bit, 2) + o // bit % 2, 2)
            bit = 2 * bit
        partners.append(peer if bit == cols else lax.rem(me + o, cols))

    def exchange(src, dst, w, span, send_sem, recv_sem):
        for peer in partners:
            pltpu.make_async_remote_copy(
                src_ref=src.at[w, block_rows(peer), span],
                dst_ref=dst.at[w, block_rows(me), span],
                send_sem=send_sem,
                recv_sem=recv_sem.at[w],
                device_id={"adapter": peer},
                device_id_type=MESH,
            ).start()
        dst[w, block_rows(me), span] = src[w, block_rows(me), span]

    def wait_exchange(dst, w, recv_sem):
        remote = dst.at[w, pl.ds(0, slots - block)]
        pltpu.make_async_copy(remote, remote, recv_sem.at[w]).wait()

    ups = owners
    dns = [n - 1 - owner for owner in owners]

    def pick(buf, k, place, owner_places, s):
        other = (place == 1) & (owner_places[s] == (0 if s == 0 else 1))
        return lax.select_n(other, buf[k, part(s), :], buf[k, part(1 if s == 0 else 0), :])

    def chosen(k):
        parts = []
        for s in range(steps):
            parts.append(
                lax.select_n(
                    owners[s] <= z,
                    pick(above, k, n - 1 - z, dns, s),
                    pick(below, k, z, ups, s),
                )
            )
        return jnp.concatenate(parts, axis=0)

    def iteration(i, carry):
        hop(below, i, z, ups, lax.rem(z + 1, n), below_sem, up_send)
        hop(above, i, n - 1 - z, dns, lax.rem(z + n - 1, n), above_sem, dn_send)

        @pl.when((lax.rem(i, group) == 0) & (i < nw))
        def _():
            p = i // group
            total = jnp.zeros((slots, pw), F32)
            for s in range(steps):
                total = total + jnp.dot(
                    pack[s], states_ref[s, :, piece_lanes(p)], preferred_element_type=F32
                )
            xout[p] = total.astype(BF16)
            exchange(xout, arrived, p, pl.ds(0, pw), x_send, x_sem)

        k = i - SKEW * (n - 1)

        @pl.when((k >= 0) & (k < nw) & (lax.rem(k, group) == 0))
        def _():
            wait_exchange(arrived, k // group, x_sem)

        @pl.when((k >= 0) & (k < nw))
        def _():
            low_acc[...] += lax.dot_general(
                arrived[k // group, :, lanes(lax.rem(k, group))],
                chosen(k),
                (((1,), (1,)), ((), ())),
                preferred_element_type=F32,
            )

        @pl.when(k == nw - 1)
        def _():
            of_row = lax.rem(lax.broadcasted_iota(jnp.int32, low.shape, 0), block) // cap
            of_col = lax.broadcasted_iota(jnp.int32, low.shape, 1) // rank
            low[...] = jnp.where(of_row == of_col, low_acc[...], 0.0).astype(BF16)

        @pl.when((k >= nw) & (k < nch))
        def _():
            w = k - nw
            dout[w // group, :, lanes(lax.rem(w, group))] = jnp.dot(
                low[...], chosen(k), preferred_element_type=F32
            ).astype(BF16)

        @pl.when((k >= nw) & (k < nch - group) & (lax.rem(k - nw, group) == group - 1))
        def _():
            exchange(dout, returned, (k - nw) // group, pl.ds(0, pw), d_send, d_sem)

        @pl.when((k >= nch - group) & (k < nch))
        def _():
            span = lanes(lax.rem(k - nw, group))
            exchange(dout, returned, pieces - 1, span, d_send, d_sem)

        w_out = k - nw - LAG

        @pl.when((w_out >= 0) & (w_out < nw) & (lax.rem(w_out, group) == group - 1))
        def _():
            p = w_out // group
            wait_exchange(returned, p, d_sem)
            for s in range(steps):
                out_ref[s, :, piece_lanes(p)] = jnp.dot(
                    unpack[s], returned[p], preferred_element_type=F32
                ).astype(BF16)

        return carry

    lax.fori_loop(0, nch + SKEW * (n - 1) + LAG, iteration, 0)

    wait_sent(below, z, up_send)
    wait_sent(above, n - 1 - z, dn_send)
    for buf, sem in ((xout, x_send), (dout, d_send)):
        sent = buf.at[:, pl.ds(0, slots - block)]
        pltpu.make_async_copy(sent, sent, sem).wait()


def body(n, cols, states, request_slot_index, down_weights, up_weights, active_adapter_owner):
    steps, rows, width = states.shape
    rank = down_weights.shape[1]
    cap = max(2, 2 * rows // cols)
    block = -(-steps * cap // 16) * 16
    slots = cols * block
    wc = min(WIDTH, width)
    nw = width // wc
    group = GROUP if nw % GROUP == 0 else 1
    vmem = pl.BlockSpec(memory_space=pltpu.VMEM)
    hbm = pl.BlockSpec(memory_space=pl.ANY)
    dma = pltpu.SemaphoreType.DMA
    stream = pltpu.VMEM((2 * nw, steps * rank, wc), BF16)
    piece = pltpu.VMEM((nw // group, slots, wc * group), BF16)
    return pl.pallas_call(
        functools.partial(kernel, n, cols, steps, cap, block, wc, group),
        out_shape=pltpu.VMEM(states.shape, states.dtype),
        in_specs=[pl.BlockSpec(memory_space=pltpu.SMEM), vmem, hbm, hbm, hbm],
        out_specs=vmem,
        scratch_shapes=[
            pltpu.VMEM(states.shape, BF16),
            pltpu.VMEM(down_weights.shape, BF16),
            pltpu.VMEM(up_weights.shape, BF16),
            stream, stream, piece, piece, piece, piece,
            pltpu.VMEM((slots, steps * rank), F32),
            pltpu.VMEM((slots, steps * rank), BF16),
            pltpu.VMEM((steps, slots, rows), BF16),
            pltpu.VMEM((steps, rows, slots), BF16),
            dma((3,)), dma, dma, dma, dma,
            dma((2 * nw,)), dma((2 * nw,)), dma((nw // group,)), dma((nw // group,)),
        ],
        compiler_params=pltpu.CompilerParams(
            collective_id=0, has_side_effects=True, vmem_limit_bytes=56 * 1024 * 1024
        ),
    )(active_adapter_owner, request_slot_index[:, :, 0], states, down_weights, up_weights)


def solution(mesh):
    return jax.shard_map(
        functools.partial(body, mesh.shape["dp"], mesh.shape["adapter"]),
        mesh=mesh,
        in_specs=(
            P(None, ("dp", "adapter"), None),
            P(None, ("dp", "adapter"), None),
            P(("dp", "adapter"), None, None),
            P(("dp", "adapter"), None, None),
            P(),
        ),
        out_specs=P(None, ("dp", "adapter"), None),
        check_vma=False,
    )
```
